128 devices in a mesh: row: 32 (over x, y, core), col: 4 (over z).
Axes of the slice: x: 4, y: 4, z: 4, core: 2. Of those that a mesh axis runs over, the one named last changes fastest.
Arguments:
- right_side: bfloat16 [65536, 4096], P(('row', 'col')), may hold values from -6 to 6
- factor: bfloat16 [65536, 2048], P(('row', 'col')), may hold values from -0.125 to 0.125
- diag_inverse: bfloat16 [2048, 512], P('col'), as said below
- tile_mask: int32 [128, 4], P(('row', 'col')), may hold values from 0 to 1, as said below
- window_rows: int32 [4], replicated, may hold values from 0 to 127, as said below
Outputs:
- solution: bfloat16 [2048, 4096], P('row', 'col')
- updated_rhs: bfloat16 [65536, 4096], P(('row', 'col'))
The draws below stay inside these ranges and needn't reach their ends.
Inputs may be any that keep to these rules, and one draw needn't show every extreme that they name: `window_rows`: distinct stored panel numbers, panels 0 and 127 always among them; panel p is stored on device p // 1 of row+col, and the window panels lie on different devices. `tile_mask`: 0 or 1; in the row of window panel k the entries of columns k and beyond are 0. `diag_inverse`: each tile is lower triangular.
All inputs are finite; a program needn't handle non-finite values.
Results may differ from the reference program's by a relative error of at most 0.0056.
Values may be sent and summed in bfloat16 or wider, within the bound.
A program may use at most 128 MiB of HBM per device.

```python
import math
import jax
import jax.numpy as jnp
from jax import lax

PANEL = 512
WIN = 4
NC = 4096
PAN_DEV = 1
NP = 128


def window_choice(key):
    holders_all = NP // PAN_DEV
    middle = 1 + jax.random.permutation(jax.random.fold_in(key, 101), holders_all - 2)[:WIN - 2]
    holders = jnp.concatenate([jnp.array([0, holders_all - 1], jnp.int32), middle.astype(jnp.int32)])
    slots = jax.random.randint(jax.random.fold_in(key, 102), (WIN,), 0, PAN_DEV).astype(jnp.int32)
    places = jnp.arange(WIN)
    slots = jnp.where(places == 0, 0, jnp.where(places == 1, PAN_DEV - 1, slots)).astype(jnp.int32)
    order = jax.random.permutation(jax.random.fold_in(key, 105), WIN)
    return (holders[order] * PAN_DEV + slots[order]).astype(jnp.int32)


def draw_window_rows(key, part):
    return window_choice(key)


def draw_tile_mask(key, part):
    window = window_choice(key)
    levels = jax.random.randint(jax.random.fold_in(key, 103), (NP, 1), 1, 5)
    picks = jax.random.randint(jax.random.fold_in(key, 104), (NP, WIN), 0, 4)
    base = (picks < levels).astype(jnp.int32)
    hits = (jnp.arange(NP)[:, None] == window[None, :]).astype(jnp.int32)
    later = (jnp.arange(WIN)[:, None] <= jnp.arange(WIN)[None, :]).astype(jnp.int32)
    forbid = jnp.minimum(jnp.dot(hits, later), 1)
    return (base * (1 - forbid)).astype(jnp.int32)


def draw_diag_inverse(key, part):
    total = WIN * PANEL
    row_pos = (jnp.arange(total) % PANEL)[:, None]
    col_pos = jnp.arange(PANEL)[None, :]
    spread = 1.2 / math.sqrt(PANEL)
    noise = jax.random.normal(jax.random.fold_in(key, 201), (total, PANEL), jnp.float32) * spread
    scales = jax.random.uniform(jax.random.fold_in(key, 202), (total, 1), jnp.float32, 0.7, 1.4)
    lower = jnp.where(col_pos < row_pos, noise, 0.0)
    full = jnp.where(col_pos == row_pos, scales, lower)
    return full.astype(jnp.bfloat16)


def block_levels(rng, extent, pieces, least, high):
    factor_of, own = 1.0, jax.random.fold_in(rng, 6)
    for dim, shards_of in pieces:
        heights = jnp.exp(jax.random.uniform(jax.random.fold_in(own, dim), (shards_of,), jnp.float32, least / len(pieces), high / len(pieces)))
        factor_of = factor_of * jnp.repeat(heights, extent[dim] // shards_of).reshape([-1 if axis == dim else 1 for axis in range(len(extent))])
    return factor_of


def bell_draw(key, extent, scale, limit, shards=(), dtype=jnp.bfloat16):
    result = jax.random.normal(key, extent, jnp.float32) * scale
    if len(shards) > 0:
        result = block_levels(key, extent, shards, -0.22, 0.18) * result
    return jnp.clip(result, min=-limit, max=limit).astype(dtype)


def setup_inputs(seed: int = 0) -> dict:
    seeds = jax.random.split(jax.random.key(seed), 6)
    right_side = bell_draw(seeds[0], (NP * PANEL, NC), 1.0, 6.0, ((0, 128),))
    factor = bell_draw(seeds[1], (NP * PANEL, WIN * PANEL), (WIN * PANEL) ** -0.5, 0.125, ((0, 128),))
    diag_inverse = draw_diag_inverse(jax.random.fold_in(seeds[5], 71), 0)
    tile_mask = draw_tile_mask(jax.random.fold_in(seeds[5], 71), 0)
    window_rows = draw_window_rows(jax.random.fold_in(seeds[5], 71), 0)
    return {"right_side": right_side, "factor": factor, "diag_inverse": diag_inverse, "tile_mask": tile_mask, "window_rows": window_rows}


def tile_term(flag, tile, panel_solution):
    zeros = jnp.zeros((tile.shape[0], panel_solution.shape[1]), jnp.float32)
    return lax.cond(flag > 0, lambda: jnp.dot(tile, panel_solution, preferred_element_type=jnp.float32), lambda: zeros)


def reference(right_side, factor, diag_inverse, tile_mask, window_rows):
    solved = []
    for k in range(WIN):
        target = window_rows[k].astype(jnp.int32)
        start = (target * PANEL).astype(jnp.int32)
        rows = lax.dynamic_slice_in_dim(right_side, start, PANEL, 0).astype(jnp.float32)
        tiles = lax.dynamic_slice_in_dim(factor, start, PANEL, 0)
        flags = lax.dynamic_slice_in_dim(tile_mask, target, 1, 0)[0]
        for j in range(k):
            rows = rows - tile_term(flags[j], tiles[:, j * PANEL:(j + 1) * PANEL], solved[j])
        rounded = rows.astype(jnp.bfloat16)
        inverse = diag_inverse[k * PANEL:(k + 1) * PANEL]
        solved.append(jnp.dot(inverse, rounded, preferred_element_type=jnp.float32).astype(jnp.bfloat16))
    whole = jnp.concatenate(solved, axis=0)

    def one_panel(item):
        rows, tiles, flags = item
        total = rows.astype(jnp.float32)
        for j in range(WIN):
            total = total - tile_term(flags[j], tiles[:, j * PANEL:(j + 1) * PANEL], whole[j * PANEL:(j + 1) * PANEL])
        return total.astype(jnp.bfloat16)

    updated = lax.map(one_panel, (right_side.reshape(NP, PANEL, NC), factor.reshape(NP, PANEL, WIN * PANEL), tile_mask))
    return whole, updated.reshape(NP * PANEL, NC)
```

```python
import jax
import jax.numpy as jnp
from jax import lax
from jax.sharding import PartitionSpec as P

AXES = ("row", "col")
NT = (((1,), (1,)), ((), ()))


def dot_nt(a, b):
    return lax.dot_general(a, b, NT, preferred_element_type=jnp.float32)


def body(right_side, factor, diag_inverse, tile_mask, window_rows):
    panel = diag_inverse.shape[1]
    window = factor.shape[1] // panel
    columns = right_side.shape[1]
    ncol = lax.axis_size("col")
    nrow = lax.axis_size("row")
    ndev = nrow * ncol
    width = columns // ndev
    col_index = lax.axis_index("col")
    row_index = lax.axis_index("row")
    me = row_index * ncol + col_index

    present = jnp.repeat(tile_mask[0] > 0, panel)
    masked = jnp.where(present[None, :], factor, jnp.zeros_like(factor))

    pieces = lax.all_to_all(
        right_side.T.reshape(ndev, width, panel), AXES, split_axis=0, concat_axis=0, tiled=True
    )

    lower = []
    for k in range(1, window):
        mine = me == window_rows[k]
        for j in range(k):
            tile = masked[:, j * panel : (j + 1) * panel]
            lower.append(jnp.where(mine, tile, jnp.zeros_like(tile)))
    lower = lax.psum(jnp.stack(lower), AXES)
    inverses = lax.all_gather(diag_inverse, "col", axis=0, tiled=True).reshape(window, panel, panel)

    solved = []
    for k in range(window):
        residual = lax.dynamic_index_in_dim(pieces, window_rows[k], 0, keepdims=False).astype(jnp.float32)
        for j in range(k):
            residual = residual - dot_nt(solved[j], lower[k * (k - 1) // 2 + j])
        solved.append(dot_nt(residual.astype(jnp.bfloat16), inverses[k]).astype(jnp.bfloat16))
    whole = lax.all_gather(jnp.concatenate(solved, axis=1), AXES, axis=0, tiled=True)

    updated = (right_side.astype(jnp.float32) - dot_nt(masked, whole)).astype(jnp.bfloat16)
    block_rows = window * panel // nrow
    block_cols = columns // ncol
    solution = lax.dynamic_slice(
        whole, (col_index * block_cols, row_index * block_rows), (block_cols, block_rows)
    ).T
    return (solution, updated)


def solution(mesh):
    in_specs = (
        P(AXES, None),
        P(AXES, None),
        P("col", None),
        P(AXES, None),
        P(),
    )
    out_specs = (P("row", "col"), P(AXES, None))
    return jax.shard_map(body, mesh=mesh, in_specs=in_specs, out_specs=out_specs, check_vma=False)
```

```python
import functools

import jax
import jax.numpy as jnp
from jax import lax
from jax.experimental import pallas as pl
from jax.experimental.pallas import tpu as pltpu
from jax.sharding import PartitionSpec as P

AXES = ("row", "col")
NT = (((1,), (1,)), ((), ()))
LANES = 128
SIDE = 4
ORDERS = ((2, 1, 0), (0, 2, 1), (1, 0, 2))


def dot_nt(a, b):
    return lax.dot_general(a, b, NT, preferred_element_type=jnp.float32)


def lane_parts(width):
    tiles = width // LANES
    sizes = [tiles // 3 + (1 if p < tiles % 3 else 0) for p in range(3)]
    starts = [sum(sizes[:p]) for p in range(3)]
    return [pl.ds(s * LANES, n * LANES) for s, n in zip(starts, sizes)]


def gather_kernel(x_ref, g_ref, local_sem, send_sem, recv_sem, side_send, side_recv):
    row, z = lax.axis_index("row"), lax.axis_index("col")
    x, y, core = row // 8, (row // 2) % 4, row % 2
    here = (x, y, z)
    parts = lane_parts(x_ref.shape[-1])

    def device(coords, c):
        return ((coords[0] * 4 + coords[1]) * 2 + c, coords[2])

    def shifted(axis, step):
        coords = list(here)
        coords[axis] = (coords[axis] + step + SIDE) % SIDE
        return coords

    partner = device(here, 1 - core)
    barrier = pltpu.get_barrier_semaphore()
    for axis in range(3):
        for step in (1, -1):
            pl.semaphore_signal(
                barrier, inc=1, device_id=device(shifted(axis, step), core),
                device_id_type=pl.DeviceIdType.MESH,
            )
    pl.semaphore_signal(barrier, inc=1, device_id=partner, device_id_type=pl.DeviceIdType.MESH)
    pl.semaphore_wait(barrier, 7)

    def block(p, f, offset, half=None):
        order = ORDERS[p]
        idx = []
        for axis in range(3):
            if axis in order[:f]:
                idx.append(pl.ds(0, SIDE))
            elif f < 3 and axis == order[f]:
                idx.append(pl.ds((here[axis] + offset + SIDE) % SIDE, 1))
            else:
                idx.append(pl.ds(here[axis], 1))
        halves = pl.ds(0, 2) if half is None else pl.ds(half, 1)
        return g_ref.at[idx[0], idx[1], pl.ds(core, 1), idx[2], halves, :, parts[p]]

    started = []

    def send(p, f, stage, way, src, dst):
        to = device(shifted(ORDERS[p][f], 1 if way == 0 else -1), core)
        copy = pltpu.make_async_remote_copy(
            src_ref=src, dst_ref=dst, send_sem=send_sem.at[p, f, stage, way],
            recv_sem=recv_sem.at[p, f, stage, way], device_id=to,
            device_id_type=pl.DeviceIdType.MESH,
        )
        copy.start()
        started.append(copy)
        return copy

    sides = []

    def hand_over(p, n, src, dst):
        copy = pltpu.make_async_remote_copy(
            src_ref=src, dst_ref=dst, send_sem=side_send.at[p, n], recv_sem=side_recv.at[p, n],
            device_id=partner, device_id_type=pl.DeviceIdType.MESH,
        )
        copy.start()
        sides.append(copy)

    first = {}
    for p in range(3):
        own = x_ref.at[:, :, :, :, :, :, parts[p]]
        first[p] = [send(p, 0, 0, way, own, block(p, 0, 0)) for way in (0, 1)]
    keep = pltpu.make_async_copy(
        x_ref, g_ref.at[pl.ds(x, 1), pl.ds(y, 1), pl.ds(core, 1), pl.ds(z, 1)], local_sem
    )
    keep.start()
    for p in range(3):
        hand_over(p, 0, x_ref.at[:, :, :, :, :, :, parts[p]], block(p, 0, 0))
    for f in range(3):
        second = {}
        for p in range(3):
            second[p] = []
            for way, offset in ((0, -1), (1, 1)):
                first[p][way].wait_recv()
                piece = block(p, f, offset, way)
                second[p].append(send(p, f, 1, way, piece, piece))
            for n, offset in ((1, -1), (2, 1)):
                whole = block(p, f, offset)
                hand_over(p, 3 * f + n, whole, whole)
        if f == 0:
            keep.wait()
        for p in range(3):
            for copy in second[p]:
                copy.wait_recv()
            if f < 2:
                own = block(p, f + 1, 0)
                first[p] = [send(p, f + 1, 0, way, own, own) for way in (0, 1)]
            far = block(p, f, 2)
            hand_over(p, 3 * f + 3, far, far)
    for copy in started:
        copy.wait_send()
    for copy in sides:
        copy.wait()


def gather_all(shard, collective_id):
    halves, rows, width = shard.shape
    return pl.pallas_call(
        gather_kernel,
        out_shape=jax.ShapeDtypeStruct((SIDE, SIDE, 2, SIDE, halves, rows, width), shard.dtype),
        in_specs=[pl.BlockSpec(memory_space=pltpu.VMEM)],
        out_specs=pl.BlockSpec(memory_space=pltpu.HBM),
        scratch_shapes=[
            pltpu.SemaphoreType.DMA,
            pltpu.SemaphoreType.DMA((3, 3, 2, 2)),
            pltpu.SemaphoreType.DMA((3, 3, 2, 2)),
            pltpu.SemaphoreType.DMA((3, 10)),
            pltpu.SemaphoreType.DMA((3, 10)),
        ],
        compiler_params=pltpu.CompilerParams(collective_id=collective_id, has_side_effects=True),
        name="gather_all_%d" % width,
    )(shard.reshape(1, 1, 1, 1, halves, rows, width))


def body(right_side, factor, diag_inverse, tile_mask, window_rows):
    panel = diag_inverse.shape[1]
    window = factor.shape[1] // panel
    columns = right_side.shape[1]
    ncol = lax.axis_size("col")
    nrow = lax.axis_size("row")
    ndev = nrow * ncol
    width = columns // ndev
    col_index = lax.axis_index("col")
    row_index = lax.axis_index("row")

    present = jnp.repeat(tile_mask[0] > 0, panel)
    masked = jnp.where(present[None, :], factor, jnp.zeros_like(factor))

    below = (window - 1) * panel
    cut = panel // nrow
    tiles = masked[:, :below].reshape(nrow, cut, ncol, below // ncol).transpose(0, 2, 1, 3)
    tiles = lax.all_to_all(
        tiles.reshape(ndev, cut, below // ncol), AXES, split_axis=0, concat_axis=0, tiled=True
    )
    pieces = lax.all_to_all(
        right_side.T.reshape(ndev, width, panel), AXES, split_axis=0, concat_axis=0, tiled=True
    )

    shard = [lax.dynamic_slice_in_dim(diag_inverse, row_index * cut, cut, 0)]
    for k in range(1, window):
        shard.append(lax.dynamic_index_in_dim(tiles, window_rows[k], 0, keepdims=False))
    shard = jnp.concatenate(shard, axis=1)
    used = shard.shape[1]
    half = -(-used // (2 * LANES)) * LANES
    shard = jnp.pad(shard, ((0, 0), (0, 2 * half - used)))
    spread = gather_all(jnp.stack([shard[:, :half], shard[:, half:]]), 0)
    spread = spread.reshape(nrow, ncol, 2, cut, half)
    spread = jnp.concatenate([spread[:, :, 0], spread[:, :, 1]], axis=3)
    inverses = spread[:, :, :, :panel].transpose(1, 0, 2, 3).reshape(window, panel, panel)
    lower = []
    for k in range(1, window):
        start = panel + (k - 1) * (below // ncol)
        part = spread[:, :, :, start : start + below // ncol]
        lower.append(part.transpose(0, 2, 1, 3).reshape(panel, below))

    solved = []
    for k in range(window):
        residual = lax.dynamic_index_in_dim(pieces, window_rows[k], 0, keepdims=False).astype(jnp.float32)
        if k > 0:
            residual = residual - dot_nt(jnp.concatenate(solved, axis=1), lower[k - 1][:, : k * panel])
        solved.append(dot_nt(residual.astype(jnp.bfloat16), inverses[k]).astype(jnp.bfloat16))
    whole = jnp.concatenate(solved, axis=1)
    whole = gather_all(whole.reshape(2, width // 2, window * panel), 1).reshape(columns, window * panel)

    updated = (right_side.astype(jnp.float32) - dot_nt(masked, whole)).astype(jnp.bfloat16)
    block_rows = window * panel // nrow
    block_cols = columns // ncol
    solution = lax.dynamic_slice(
        whole, (col_index * block_cols, row_index * block_rows), (block_cols, block_rows)
    ).T
    return (solution, updated)


def solution(mesh):
    in_specs = (
        P(AXES, None),
        P(AXES, None),
        P("col", None),
        P(AXES, None),
        P(),
    )
    out_specs = (P("row", "col"), P(AXES, None))
    return jax.shard_map(body, mesh=mesh, in_specs=in_specs, out_specs=out_specs, check_vma=False)
```

```python
import functools

import jax
import jax.numpy as jnp
from jax import lax
from jax.experimental import pallas as pl
from jax.experimental.pallas import tpu as pltpu
from jax.sharding import PartitionSpec as P

AXES = ("row", "col")
NT = (((1,), (1,)), ((), ()))
LANES = 128
SIDE = 4
ORDERS = ((2, 1, 0), (0, 2, 1), (1, 0, 2))


def dot_nt(a, b):
    return lax.dot_general(a, b, NT, preferred_element_type=jnp.float32)


def lane_parts(width):
    tiles = width // LANES
    sizes = [tiles // 3 + (1 if p < tiles % 3 else 0) for p in range(3)]
    starts = [sum(sizes[:p]) for p in range(3)]
    return [pl.ds(s * LANES, n * LANES) for s, n in zip(starts, sizes)]


def gather_kernel(x_ref, g_ref, local_sem, send_sem, recv_sem, side_send, side_recv):
    row, z = lax.axis_index("row"), lax.axis_index("col")
    x, y, core = row // 8, (row // 2) % 4, row % 2
    here = (x, y, z)
    parts = lane_parts(x_ref.shape[-1])

    def device(coords, c):
        return ((coords[0] * 4 + coords[1]) * 2 + c, coords[2])

    def shifted(axis, step):
        coords = list(here)
        coords[axis] = (coords[axis] + step + SIDE) % SIDE
        return coords

    partner = device(here, 1 - core)
    barrier = pltpu.get_barrier_semaphore()
    for axis in range(3):
        for step in (1, -1):
            pl.semaphore_signal(
                barrier, inc=1, device_id=device(shifted(axis, step), core),
                device_id_type=pl.DeviceIdType.MESH,
            )
    pl.semaphore_signal(barrier, inc=1, device_id=partner, device_id_type=pl.DeviceIdType.MESH)
    pl.semaphore_wait(barrier, 7)

    def block(p, f, offset, half=None):
        order = ORDERS[p]
        idx = []
        for axis in range(3):
            if axis in order[:f]:
                idx.append(pl.ds(0, SIDE))
            elif f < 3 and axis == order[f]:
                idx.append(pl.ds((here[axis] + offset + SIDE) % SIDE, 1))
            else:
                idx.append(pl.ds(here[axis], 1))
        halves = pl.ds(0, 2) if half is None else pl.ds(half, 1)
        return g_ref.at[idx[0], idx[1], pl.ds(core, 1), idx[2], halves, :, parts[p]]

    started = []

    def send(p, f, stage, way, src, dst):
        to = device(shifted(ORDERS[p][f], 1 if way == 0 else -1), core)
        copy = pltpu.make_async_remote_copy(
            src_ref=src, dst_ref=dst, send_sem=send_sem.at[p, f, stage, way],
            recv_sem=recv_sem.at[p, f, stage, way], device_id=to,
            device_id_type=pl.DeviceIdType.MESH,
        )
        copy.start()
        started.append(copy)
        return copy

    sides = []

    def hand_over(p, n, src, dst):
        copy = pltpu.make_async_remote_copy(
            src_ref=src, dst_ref=dst, send_sem=side_send.at[p, n], recv_sem=side_recv.at[p, n],
            device_id=partner, device_id_type=pl.DeviceIdType.MESH,
        )
        copy.start()
        sides.append(copy)

    def send_halves(p, f, halves):
        copies = {}
        for n in range(2):
            for way in (0, 1):
                half = way if n == 0 else 1 - way
                copies[way, n] = send(p, f, n, way, halves(half), block(p, f, 0, half))
        return copies

    first = {}
    for p in range(3):
        first[p] = send_halves(
            p, 0, lambda half: x_ref.at[:, :, :, :, pl.ds(half, 1), :, parts[p]]
        )
    keep = pltpu.make_async_copy(
        x_ref, g_ref.at[pl.ds(x, 1), pl.ds(y, 1), pl.ds(core, 1), pl.ds(z, 1)], local_sem
    )
    keep.start()
    for p in range(3):
        hand_over(p, 0, x_ref.at[:, :, :, :, :, :, parts[p]], block(p, 0, 0))
    for f in range(3):
        second = {}
        for p in range(3):
            second[p] = []
            for way, offset in ((0, -1), (1, 1)):
                first[p][way, 0].wait_recv()
                piece = block(p, f, offset, way)
                second[p].append(send(p, f, 2, way, piece, piece))
        for p in range(3):
            for way, offset in ((0, -1), (1, 1)):
                first[p][way, 1].wait_recv()
                whole = block(p, f, offset)
                hand_over(p, 3 * f + 1 + way, whole, whole)
        if f == 0:
            keep.wait()
        for p in range(3):
            for copy in second[p]:
                copy.wait_recv()
            if f < 2:
                first[p] = send_halves(p, f + 1, lambda half: block(p, f + 1, 0, half))
            far = block(p, f, 2)
            hand_over(p, 3 * f + 3, far, far)
    for copy in started:
        copy.wait_send()
    for copy in sides:
        copy.wait()


def gather_all(shard, collective_id):
    halves, rows, width = shard.shape
    return pl.pallas_call(
        gather_kernel,
        out_shape=jax.ShapeDtypeStruct((SIDE, SIDE, 2, SIDE, halves, rows, width), shard.dtype),
        in_specs=[pl.BlockSpec(memory_space=pltpu.VMEM)],
        out_specs=pl.BlockSpec(memory_space=pltpu.HBM),
        scratch_shapes=[
            pltpu.SemaphoreType.DMA,
            pltpu.SemaphoreType.DMA((3, 3, 3, 2)),
            pltpu.SemaphoreType.DMA((3, 3, 3, 2)),
            pltpu.SemaphoreType.DMA((3, 10)),
            pltpu.SemaphoreType.DMA((3, 10)),
        ],
        compiler_params=pltpu.CompilerParams(collective_id=collective_id, has_side_effects=True),
        name="gather_all_%d" % width,
    )(shard.reshape(1, 1, 1, 1, halves, rows, width))


def cut_kernel(mask_ref, f_ref, o_ref):
    groups, below = o_ref.shape[0], f_ref.shape[1]
    ncol = o_ref.shape[1]
    cut, span = o_ref.shape[2:]
    kept = jnp.where(mask_ref[:, :below] > 0, f_ref[...], jnp.zeros_like(f_ref))
    for g in range(groups):
        for c in range(ncol):
            o_ref[g, c] = kept[g * cut : (g + 1) * cut, c * span : (c + 1) * span]


def cut_tiles(factor, present, below, nrow, ncol):
    panel = factor.shape[0]
    cut, span, steps = panel // nrow, below // ncol, 4
    return pl.pallas_call(
        cut_kernel,
        grid=(steps,),
        out_shape=jax.ShapeDtypeStruct((nrow, ncol, cut, span), factor.dtype),
        in_specs=[
            pl.BlockSpec(present.shape, lambda i: (0, 0)),
            pl.BlockSpec((panel // steps, below), lambda i: (i, 0)),
        ],
        out_specs=pl.BlockSpec((nrow // steps, ncol, cut, span), lambda i: (i, 0, 0, 0)),
        name="cut_tiles",
    )(present, factor)


def solve_kernel(rows_ref, pieces_ref, g_ref, o_ref, r_buf, d_buf, l_buf, r_sem, d_sem, l_sem):
    window, _, panel = r_buf.shape
    span = l_buf.shape[-1] // SIDE
    right, inverse, lower = [], [], []
    for k in range(window):
        copy = pltpu.make_async_copy(pieces_ref.at[rows_ref[k]], r_buf.at[k], r_sem.at[k])
        copy.start()
        right.append(copy)
        copy = pltpu.make_async_copy(
            g_ref.at[:, :, :, k, 0, :, pl.ds(0, panel)], d_buf.at[k], d_sem.at[k]
        )
        copy.start()
        inverse.append(copy)
        if k == 0:
            continue
        half, lane = divmod(panel + (k - 1) * span, g_ref.shape[-1])
        for z in range(SIDE):
            copy = pltpu.make_async_copy(
                g_ref.at[:, :, :, z, half, :, pl.ds(lane, span)],
                l_buf.at[k - 1, :, :, :, :, pl.ds(z * span, span)],
                l_sem.at[k - 1, z],
            )
            copy.start()
            lower.append(copy)
    for k in range(window):
        right[k].wait()
        residual = r_buf[k].astype(jnp.float32)
        if k > 0:
            for z in range(SIDE):
                lower[(k - 1) * SIDE + z].wait()
            tiles = l_buf[k - 1].reshape(panel, SIDE * span)
            residual = residual - dot_nt(o_ref[:, : k * panel], tiles[:, : k * panel])
        inverse[k].wait()
        inv = d_buf[k].reshape(panel, panel)
        o_ref[:, k * panel : (k + 1) * panel] = dot_nt(residual.astype(jnp.bfloat16), inv).astype(
            jnp.bfloat16
        )


def solve(window_rows, pieces, spread):
    _, width, panel = pieces.shape
    window = window_rows.shape[0]
    cut = spread.shape[5]
    below = (window - 1) * panel
    return pl.pallas_call(
        solve_kernel,
        out_shape=jax.ShapeDtypeStruct((width, window * panel), pieces.dtype),
        in_specs=[
            pl.BlockSpec(memory_space=pltpu.SMEM),
            pl.BlockSpec(memory_space=pl.ANY),
            pl.BlockSpec(memory_space=pl.ANY),
        ],
        out_specs=pl.BlockSpec(memory_space=pltpu.VMEM),
        scratch_shapes=[
            pltpu.VMEM((window, width, panel), pieces.dtype),
            pltpu.VMEM((window, SIDE, SIDE, 2, cut, panel), pieces.dtype),
            pltpu.VMEM((window - 1, SIDE, SIDE, 2, cut, below), pieces.dtype),
            pltpu.SemaphoreType.DMA((window,)),
            pltpu.SemaphoreType.DMA((window,)),
            pltpu.SemaphoreType.DMA((window - 1, SIDE)),
        ],
        name="solve_window",
    )(window_rows, pieces, spread)


def body(right_side, factor, diag_inverse, tile_mask, window_rows):
    panel = diag_inverse.shape[1]
    window = factor.shape[1] // panel
    columns = right_side.shape[1]
    ncol = lax.axis_size("col")
    nrow = lax.axis_size("row")
    ndev = nrow * ncol
    width = columns // ndev
    col_index = lax.axis_index("col")
    row_index = lax.axis_index("row")

    present = jnp.repeat(tile_mask[0] > 0, panel)
    masked = jnp.where(present[None, :], factor, jnp.zeros_like(factor))

    below = (window - 1) * panel
    cut = panel // nrow
    kept = present[None, :].astype(factor.dtype)
    tiles = cut_tiles(factor, kept, below, nrow, ncol)
    tiles = lax.all_to_all(
        tiles.reshape(ndev, cut, below // ncol), AXES, split_axis=0, concat_axis=0, tiled=True
    )
    pieces = lax.all_to_all(
        right_side.T.reshape(ndev, width, panel), AXES, split_axis=0, concat_axis=0, tiled=True
    )

    shard = [lax.dynamic_slice_in_dim(diag_inverse, row_index * cut, cut, 0)]
    for k in range(1, window):
        shard.append(lax.dynamic_index_in_dim(tiles, window_rows[k], 0, keepdims=False))
    shard = jnp.concatenate(shard, axis=1)
    used = shard.shape[1]
    half = -(-used // (2 * LANES)) * LANES
    shard = jnp.pad(shard, ((0, 0), (0, 2 * half - used)))
    spread = gather_all(jnp.stack([shard[:, :half], shard[:, half:]]), 0)
    whole = solve(window_rows, pieces, spread)
    whole = gather_all(whole.reshape(2, width // 2, window * panel), 1).reshape(columns, window * panel)

    updated = (right_side.astype(jnp.float32) - dot_nt(masked, whole)).astype(jnp.bfloat16)
    block_rows = window * panel // nrow
    block_cols = columns // ncol
    solution = lax.dynamic_slice(
        whole, (col_index * block_cols, row_index * block_rows), (block_cols, block_rows)
    ).T
    return (solution, updated)


def solution(mesh):
    in_specs = (
        P(AXES, None),
        P(AXES, None),
        P("col", None),
        P(AXES, None),
        P(),
    )
    out_specs = (P("row", "col"), P(AXES, None))
    return jax.shard_map(body, mesh=mesh, in_specs=in_specs, out_specs=out_specs, check_vma=False)
```

```python
import functools

import jax
import jax.numpy as jnp
from jax import lax
from jax.experimental import pallas as pl
from jax.experimental.pallas import tpu as pltpu
from jax.sharding import PartitionSpec as P

AXES = ("row", "col")
NT = (((1,), (1,)), ((), ()))
LANES = 128
SIDE = 4
SUBS = (0, -1, 1, 2)
ORDERS = ((2, 1, 0), (0, 2, 1), (1, 0, 2))


def dot_nt(a, b):
    return lax.dot_general(a, b, NT, preferred_element_type=jnp.float32)


def lane_parts(width):
    tiles = width // LANES
    sizes = [tiles // 3 + (1 if p < tiles % 3 else 0) for p in range(3)]
    starts = [sum(sizes[:p]) for p in range(3)]
    return [pl.ds(s * LANES, n * LANES) for s, n in zip(starts, sizes)]


def gather_kernel(x_ref, g_ref, local_sem, send_sem, recv_sem, side_send, side_recv):
    row, z = lax.axis_index("row"), lax.axis_index("col")
    x, y, core = row // 8, (row // 2) % 4, row % 2
    here = (x, y, z)
    parts = lane_parts(x_ref.shape[-1])

    def device(coords, c):
        return ((coords[0] * 4 + coords[1]) * 2 + c, coords[2])

    def shifted(axis, step):
        coords = list(here)
        coords[axis] = (coords[axis] + step + SIDE) % SIDE
        return coords

    partner = device(here, 1 - core)
    barrier = pltpu.get_barrier_semaphore()
    for axis in range(3):
        for step in (1, -1):
            pl.semaphore_signal(
                barrier, inc=1, device_id=device(shifted(axis, step), core),
                device_id_type=pl.DeviceIdType.MESH,
            )
    pl.semaphore_signal(barrier, inc=1, device_id=partner, device_id_type=pl.DeviceIdType.MESH)
    pl.semaphore_wait(barrier, 7)

    def block(p, f, offset, half=None, sub=None):
        order = ORDERS[p]
        idx = []
        for axis in range(3):
            if axis == order[f]:
                idx.append(pl.ds((here[axis] + offset + SIDE) % SIDE, 1))
            elif axis in order[:f] and (sub is None or axis != order[f - 1]):
                idx.append(pl.ds(0, SIDE))
            else:
                idx.append(pl.ds((here[axis] + (sub or 0) + SIDE) % SIDE if axis in order[:f] else here[axis], 1))
        halves = pl.ds(0, 2) if half is None else pl.ds(half, 1)
        return g_ref.at[idx[0], idx[1], pl.ds(core, 1), idx[2], halves, :, parts[p]]

    started = []

    def send(p, f, n, stage, way, src, dst):
        to = device(shifted(ORDERS[p][f], 1 if way == 0 else -1), core)
        copy = pltpu.make_async_remote_copy(
            src_ref=src, dst_ref=dst, send_sem=send_sem.at[p, f, n, stage, way],
            recv_sem=recv_sem.at[p, f, n, stage, way], device_id=to,
            device_id_type=pl.DeviceIdType.MESH,
        )
        copy.start()
        started.append(copy)
        return copy

    sides = []

    def hand_over(p, n, src, dst):
        copy = pltpu.make_async_remote_copy(
            src_ref=src, dst_ref=dst, send_sem=side_send.at[p, n], recv_sem=side_recv.at[p, n],
            device_id=partner, device_id_type=pl.DeviceIdType.MESH,
        )
        copy.start()
        sides.append(copy)

    first = {}

    def send_halves(p, f, n):
        sub = SUBS[n] if f > 0 else None
        for stage in range(2):
            for way in (0, 1):
                half = way if stage == 0 else 1 - way
                dst = block(p, f, 0, half, sub)
                if f == 0 or (f == 1 and n == 0):
                    src = x_ref.at[:, :, :, :, pl.ds(half, 1), :, parts[p]]
                else:
                    src = dst
                first[p, f, n, stage, way] = send(p, f, n, stage, way, src, dst)

    for p in range(3):
        send_halves(p, 0, 0)
    keep = pltpu.make_async_copy(
        x_ref, g_ref.at[pl.ds(x, 1), pl.ds(y, 1), pl.ds(core, 1), pl.ds(z, 1)], local_sem
    )
    keep.start()
    for p in range(3):
        hand_over(p, 0, x_ref.at[:, :, :, :, :, :, parts[p]], block(p, 0, 0))
    sides_of = ((0, -1), (1, 1))
    for f in range(3):
        if f == 1:
            keep.wait()
        if f < 2:
            for p in range(3):
                send_halves(p, f + 1, 0)
        second = {}
        for n in range(len(SUBS) if f > 0 else 1):
            sub = SUBS[n] if f > 0 else None
            for p in range(3):
                for way, offset in sides_of:
                    first[p, f, n, 0, way].wait_recv()
                    piece = block(p, f, offset, way, sub)
                    second[p, n, way] = send(p, f, n, 2, way, piece, piece)
            for p in range(3):
                for way, offset in sides_of:
                    first[p, f, n, 1, way].wait_recv()
        for p in range(3):
            if f < 2:
                send_halves(p, f + 1, 1)
                send_halves(p, f + 1, 2)
            for way, offset in sides_of:
                whole = block(p, f, offset)
                hand_over(p, 3 * f + 1 + way, whole, whole)
        for p in range(3):
            for key, copy in second.items():
                if key[0] == p:
                    copy.wait_recv()
            if f < 2:
                send_halves(p, f + 1, 3)
            far = block(p, f, 2)
            hand_over(p, 3 * f + 3, far, far)
    for copy in started:
        copy.wait_send()
    for copy in sides:
        copy.wait()


def gather_all(shard, collective_id):
    halves, rows, width = shard.shape
    return pl.pallas_call(
        gather_kernel,
        out_shape=jax.ShapeDtypeStruct((SIDE, SIDE, 2, SIDE, halves, rows, width), shard.dtype),
        in_specs=[pl.BlockSpec(memory_space=pltpu.VMEM)],
        out_specs=pl.BlockSpec(memory_space=pltpu.HBM),
        scratch_shapes=[
            pltpu.SemaphoreType.DMA,
            pltpu.SemaphoreType.DMA((3, 3, 4, 3, 2)),
            pltpu.SemaphoreType.DMA((3, 3, 4, 3, 2)),
            pltpu.SemaphoreType.DMA((3, 10)),
            pltpu.SemaphoreType.DMA((3, 10)),
        ],
        compiler_params=pltpu.CompilerParams(collective_id=collective_id, has_side_effects=True),
        name="gather_all_%d" % width,
    )(shard.reshape(1, 1, 1, 1, halves, rows, width))


def keep_present(mask_ref, f_ref, count):
    panel = f_ref.shape[1] // count
    tiles = []
    for j in range(count):
        tile = f_ref[:, j * panel : (j + 1) * panel]
        tiles.append(jnp.where(mask_ref[0, j] > 0, tile, jnp.zeros_like(tile)))
    return jnp.concatenate(tiles, axis=1)


def cut_kernel(mask_ref, f_ref, o_ref):
    groups, ncol, cut, span = o_ref.shape
    kept = keep_present(mask_ref, f_ref, mask_ref.shape[1] - 1)
    for g in range(groups):
        for c in range(ncol):
            o_ref[g, c] = kept[g * cut : (g + 1) * cut, c * span : (c + 1) * span]


def cut_tiles(factor, tile_mask, below, nrow, ncol):
    panel = factor.shape[0]
    cut, span, steps = panel // nrow, below // ncol, 4
    return pl.pallas_call(
        cut_kernel,
        grid=(steps,),
        out_shape=jax.ShapeDtypeStruct((nrow, ncol, cut, span), factor.dtype),
        in_specs=[
            pl.BlockSpec(memory_space=pltpu.SMEM),
            pl.BlockSpec((panel // steps, below), lambda i: (i, 0)),
        ],
        out_specs=pl.BlockSpec((nrow // steps, ncol, cut, span), lambda i: (i, 0, 0, 0)),
        name="cut_tiles",
    )(tile_mask, factor)


def solve_kernel(rows_ref, pieces_ref, g_ref, o_ref, r_buf, d_buf, l_buf, r_sem, d_sem, l_sem):
    window, _, panel = r_buf.shape
    span = l_buf.shape[-1] // SIDE
    right, inverse, lower = [], [], []
    for k in range(window):
        copy = pltpu.make_async_copy(pieces_ref.at[rows_ref[k]], r_buf.at[k], r_sem.at[k])
        copy.start()
        right.append(copy)
        copy = pltpu.make_async_copy(
            g_ref.at[:, :, :, k, 0, :, pl.ds(0, panel)], d_buf.at[k], d_sem.at[k]
        )
        copy.start()
        inverse.append(copy)
        if k == 0:
            continue
        half, lane = divmod(panel + (k - 1) * span, g_ref.shape[-1])
        for z in range(SIDE):
            copy = pltpu.make_async_copy(
                g_ref.at[:, :, :, z, half, :, pl.ds(lane, span)],
                l_buf.at[k - 1, :, :, :, :, pl.ds(z * span, span)],
                l_sem.at[k - 1, z],
            )
            copy.start()
            lower.append(copy)
    for k in range(window):
        right[k].wait()
        residual = r_buf[k].astype(jnp.float32)
        if k > 0:
            for z in range(SIDE):
                lower[(k - 1) * SIDE + z].wait()
            tiles = l_buf[k - 1].reshape(panel, SIDE * span)
            residual = residual - dot_nt(o_ref[:, : k * panel], tiles[:, : k * panel])
        inverse[k].wait()
        inv = d_buf[k].reshape(panel, panel)
        o_ref[:, k * panel : (k + 1) * panel] = dot_nt(residual.astype(jnp.bfloat16), inv).astype(
            jnp.bfloat16
        )


def solve(window_rows, pieces, spread):
    _, width, panel = pieces.shape
    window = window_rows.shape[0]
    cut = spread.shape[5]
    below = (window - 1) * panel
    return pl.pallas_call(
        solve_kernel,
        out_shape=jax.ShapeDtypeStruct((width, window * panel), pieces.dtype),
        in_specs=[
            pl.BlockSpec(memory_space=pltpu.SMEM),
            pl.BlockSpec(memory_space=pl.ANY),
            pl.BlockSpec(memory_space=pl.ANY),
        ],
        out_specs=pl.BlockSpec(memory_space=pltpu.VMEM),
        scratch_shapes=[
            pltpu.VMEM((window, width, panel), pieces.dtype),
            pltpu.VMEM((window, SIDE, SIDE, 2, cut, panel), pieces.dtype),
            pltpu.VMEM((window - 1, SIDE, SIDE, 2, cut, below), pieces.dtype),
            pltpu.SemaphoreType.DMA((window,)),
            pltpu.SemaphoreType.DMA((window,)),
            pltpu.SemaphoreType.DMA((window - 1, SIDE)),
        ],
        name="solve_window",
    )(window_rows, pieces, spread)


def update_kernel(place_ref, mask_ref, r_ref, f_ref, w_ref, s_ref, o_ref, kept_ref):
    step = pl.program_id(0)

    @pl.when(step == 0)
    def _():
        kept_ref[...] = keep_present(mask_ref, f_ref, mask_ref.shape[1])

    removed = dot_nt(kept_ref[...], w_ref[...])
    o_ref[...] = (r_ref[...].astype(jnp.float32) - removed).astype(o_ref.dtype)

    @pl.when(step == place_ref[1])
    def _():
        rows = s_ref.shape[0]
        per = LANES // rows
        lane = pl.multiple_of(place_ref[0] // per * LANES, LANES)
        tile = w_ref[:, pl.ds(lane, LANES)].astype(jnp.float32).T
        mine = tile[:rows]
        for n in range(1, per):
            mine = jnp.where(place_ref[0] % per == n, tile[n * rows : (n + 1) * rows], mine)
        s_ref[...] = mine.astype(s_ref.dtype)


def update(place, tile_mask, right_side, factor, whole, nrow, ncol):
    panel, columns = right_side.shape
    step = columns // ncol
    rows = factor.shape[1] // nrow
    return pl.pallas_call(
        update_kernel,
        grid=(ncol,),
        out_shape=(
            jax.ShapeDtypeStruct((rows, step), whole.dtype),
            jax.ShapeDtypeStruct(right_side.shape, right_side.dtype),
        ),
        in_specs=[
            pl.BlockSpec(memory_space=pltpu.SMEM),
            pl.BlockSpec(memory_space=pltpu.SMEM),
            pl.BlockSpec((panel, step), lambda i: (0, i)),
            pl.BlockSpec(factor.shape, lambda i: (0, 0), pipeline_mode=pl.Buffered(1)),
            pl.BlockSpec((step, factor.shape[1]), lambda i: (i, 0)),
        ],
        out_specs=(
            pl.BlockSpec((rows, step), lambda i: (0, 0)),
            pl.BlockSpec((panel, step), lambda i: (0, i)),
        ),
        scratch_shapes=[pltpu.VMEM(factor.shape, factor.dtype)],
        name="update_panel",
    )(place, tile_mask, right_side, factor, whole)


def body(right_side, factor, diag_inverse, tile_mask, window_rows):
    panel = diag_inverse.shape[1]
    window = factor.shape[1] // panel
    columns = right_side.shape[1]
    ncol = lax.axis_size("col")
    nrow = lax.axis_size("row")
    ndev = nrow * ncol
    width = columns // ndev
    col_index = lax.axis_index("col")
    row_index = lax.axis_index("row")

    below = (window - 1) * panel
    cut = panel // nrow
    tiles = cut_tiles(factor, tile_mask, below, nrow, ncol)
    tiles = lax.all_to_all(
        tiles.reshape(ndev, cut, below // ncol), AXES, split_axis=0, concat_axis=0, tiled=True
    )
    pieces = lax.all_to_all(
        right_side.T.reshape(ndev, width, panel), AXES, split_axis=0, concat_axis=0, tiled=True
    )

    shard = [lax.dynamic_slice_in_dim(diag_inverse, row_index * cut, cut, 0)]
    for k in range(1, window):
        shard.append(lax.dynamic_index_in_dim(tiles, window_rows[k], 0, keepdims=False))
    shard = jnp.concatenate(shard, axis=1)
    used = shard.shape[1]
    half = -(-used // (2 * LANES)) * LANES
    shard = jnp.pad(shard, ((0, 0), (0, 2 * half - used)))
    spread = gather_all(jnp.stack([shard[:, :half], shard[:, half:]]), 0)
    whole = solve(window_rows, pieces, spread)
    whole = gather_all(whole.reshape(2, width // 2, window * panel), 1).reshape(columns, window * panel)

    place = jnp.stack([row_index, col_index]).astype(jnp.int32)
    solution, updated = update(place, tile_mask, right_side, factor, whole, nrow, ncol)
    return (solution, updated)


def solution(mesh):
    in_specs = (
        P(AXES, None),
        P(AXES, None),
        P("col", None),
        P(AXES, None),
        P(),
    )
    out_specs = (P("row", "col"), P(AXES, None))
    return jax.shard_map(body, mesh=mesh, in_specs=in_specs, out_specs=out_specs, check_vma=False)
```

```python
import functools

import jax
import jax.numpy as jnp
from jax import lax
from jax.experimental import pallas as pl
from jax.experimental.pallas import tpu as pltpu
from jax.sharding import PartitionSpec as P

AXES = ("row", "col")
NT = (((1,), (1,)), ((), ()))
LANES = 128
SIDE = 4
SUBS = (0, -1, 1, 2)
ORDERS = ((2, 1, 0), (0, 2, 1), (1, 0, 2))


def dot_nt(a, b):
    return lax.dot_general(a, b, NT, preferred_element_type=jnp.float32)


def lane_parts(width):
    tiles = width // LANES
    sizes = [tiles // 3 + (1 if p < tiles % 3 else 0) for p in range(3)]
    starts = [sum(sizes[:p]) for p in range(3)]
    return [pl.ds(s * LANES, n * LANES) for s, n in zip(starts, sizes)]


def gather_kernel(x_ref, g_ref, local_sem, send_sem, recv_sem, side_send, side_recv):
    row, z = lax.axis_index("row"), lax.axis_index("col")
    x, y, core = row // 8, (row // 2) % 4, row % 2
    here = (x, y, z)
    parts = lane_parts(x_ref.shape[-1])

    def device(coords, c):
        return ((coords[0] * 4 + coords[1]) * 2 + c, coords[2])

    def shifted(axis, step):
        coords = list(here)
        coords[axis] = (coords[axis] + step + SIDE) % SIDE
        return coords

    partner = device(here, 1 - core)
    barrier = pltpu.get_barrier_semaphore()
    for axis in range(3):
        for step in (1, -1):
            pl.semaphore_signal(
                barrier, inc=1, device_id=device(shifted(axis, step), core),
                device_id_type=pl.DeviceIdType.MESH,
            )
    pl.semaphore_signal(barrier, inc=1, device_id=partner, device_id_type=pl.DeviceIdType.MESH)
    pl.semaphore_wait(barrier, 7)

    def block(p, f, offset, half=None, sub=None):
        order = ORDERS[p]
        idx = []
        for axis in range(3):
            if axis == order[f]:
                idx.append(pl.ds((here[axis] + offset + SIDE) % SIDE, 1))
            elif axis in order[:f] and (sub is None or axis != order[f - 1]):
                idx.append(pl.ds(0, SIDE))
            else:
                idx.append(pl.ds((here[axis] + (sub or 0) + SIDE) % SIDE if axis in order[:f] else here[axis], 1))
        halves = pl.ds(0, 2) if half is None else pl.ds(half, 1)
        return g_ref.at[idx[0], idx[1], pl.ds(core, 1), idx[2], halves, :, parts[p]]

    started = []

    def send(p, f, n, stage, way, src, dst):
        to = device(shifted(ORDERS[p][f], 1 if way == 0 else -1), core)
        copy = pltpu.make_async_remote_copy(
            src_ref=src, dst_ref=dst, send_sem=send_sem.at[p, f, n, stage, way],
            recv_sem=recv_sem.at[p, f, n, stage, way], device_id=to,
            device_id_type=pl.DeviceIdType.MESH,
        )
        copy.start()
        started.append(copy)
        return copy

    sides = []

    def hand_over(p, n, src, dst):
        copy = pltpu.make_async_remote_copy(
            src_ref=src, dst_ref=dst, send_sem=side_send.at[p, n], recv_sem=side_recv.at[p, n],
            device_id=partner, device_id_type=pl.DeviceIdType.MESH,
        )
        copy.start()
        sides.append(copy)

    first = {}

    def send_halves(p, f, n):
        sub = SUBS[n] if f > 0 else None
        for stage in range(2):
            for way in (0, 1):
                half = way if stage == 0 else 1 - way
                dst = block(p, f, 0, half, sub)
                if f == 0 or (f == 1 and n == 0):
                    src = x_ref.at[:, :, :, :, pl.ds(half, 1), :, parts[p]]
                else:
                    src = dst
                first[p, f, n, stage, way] = send(p, f, n, stage, way, src, dst)

    for p in range(3):
        send_halves(p, 0, 0)
    keep = pltpu.make_async_copy(
        x_ref, g_ref.at[pl.ds(x, 1), pl.ds(y, 1), pl.ds(core, 1), pl.ds(z, 1)], local_sem
    )
    keep.start()
    for p in range(3):
        hand_over(p, 0, x_ref.at[:, :, :, :, :, :, parts[p]], block(p, 0, 0))
    sides_of = ((0, -1), (1, 1))
    for f in range(3):
        if f == 1:
            keep.wait()
        if f < 2:
            for p in range(3):
                send_halves(p, f + 1, 0)
        second = {}
        for n in range(len(SUBS) if f > 0 else 1):
            sub = SUBS[n] if f > 0 else None
            for p in range(3):
                for way, offset in sides_of:
                    first[p, f, n, 0, way].wait_recv()
                    piece = block(p, f, offset, way, sub)
                    second[p, n, way] = send(p, f, n, 2, way, piece, piece)
            for p in range(3):
                for way, offset in sides_of:
                    first[p, f, n, 1, way].wait_recv()
        for p in range(3):
            if f < 2:
                send_halves(p, f + 1, 1)
                send_halves(p, f + 1, 2)
            for way, offset in sides_of:
                whole = block(p, f, offset)
                hand_over(p, 3 * f + 1 + way, whole, whole)
        for p in range(3):
            for key, copy in second.items():
                if key[0] == p:
                    copy.wait_recv()
            if f < 2:
                send_halves(p, f + 1, 3)
            far = block(p, f, 2)
            hand_over(p, 3 * f + 3, far, far)
    for copy in started:
        copy.wait_send()
    for copy in sides:
        copy.wait()


def gather_all(shard, collective_id):
    halves, rows, width = shard.shape
    return pl.pallas_call(
        gather_kernel,
        out_shape=jax.ShapeDtypeStruct((SIDE, SIDE, 2, SIDE, halves, rows, width), shard.dtype),
        in_specs=[pl.BlockSpec(memory_space=pltpu.VMEM)],
        out_specs=pl.BlockSpec(memory_space=pltpu.HBM),
        scratch_shapes=[
            pltpu.SemaphoreType.DMA,
            pltpu.SemaphoreType.DMA((3, 3, 4, 3, 2)),
            pltpu.SemaphoreType.DMA((3, 3, 4, 3, 2)),
            pltpu.SemaphoreType.DMA((3, 10)),
            pltpu.SemaphoreType.DMA((3, 10)),
        ],
        compiler_params=pltpu.CompilerParams(collective_id=collective_id, has_side_effects=True),
        name="gather_all_%d" % width,
    )(shard.reshape(1, 1, 1, 1, halves, rows, width))


def keep_present(mask_ref, f_ref, count):
    panel = f_ref.shape[1] // count
    tiles = []
    for j in range(count):
        tile = f_ref[:, j * panel : (j + 1) * panel]
        tiles.append(jnp.where(mask_ref[0, j] > 0, tile, jnp.zeros_like(tile)))
    return jnp.concatenate(tiles, axis=1)


def cut_kernel(mask_ref, f_ref, o_ref):
    groups, ncol, cut, span = o_ref.shape
    count = mask_ref.shape[1] - 1
    panel, lanes = f_ref.shape[1] // count, span // count
    kept = keep_present(mask_ref, f_ref, count)
    for g in range(groups):
        for c in range(ncol):
            rows = kept[g * cut : (g + 1) * cut]
            o_ref[g, c] = jnp.concatenate(
                [rows[:, j * panel + c * lanes : j * panel + (c + 1) * lanes] for j in range(count)],
                axis=1,
            )


def cut_tiles(factor, tile_mask, below, nrow, ncol):
    panel = factor.shape[0]
    cut, span, steps = panel // nrow, below // ncol, 4
    return pl.pallas_call(
        cut_kernel,
        grid=(steps,),
        out_shape=jax.ShapeDtypeStruct((nrow, ncol, cut, span), factor.dtype),
        in_specs=[
            pl.BlockSpec(memory_space=pltpu.SMEM),
            pl.BlockSpec((panel // steps, below), lambda i: (i, 0)),
        ],
        out_specs=pl.BlockSpec((nrow // steps, ncol, cut, span), lambda i: (i, 0, 0, 0)),
        name="cut_tiles",
    )(tile_mask, factor)


def pack_kernel(rows_ref, tiles_ref, inverse_ref, o_ref, d_buf, sem):
    count = rows_ref.shape[0] - 1
    _, cut, span = tiles_ref.shape
    lanes = span // count
    start = pl.multiple_of(lax.axis_index("row") * cut, cut)
    copy = pltpu.make_async_copy(inverse_ref.at[pl.ds(start, cut)], d_buf, sem)
    copy.start()
    pieces = [tiles_ref[rows_ref[k]][:, : k * lanes] for k in range(1, count + 1)]
    copy.wait()
    packed = [d_buf[...]] + pieces
    packed = jnp.concatenate(packed, axis=1)
    half = o_ref.shape[-1]
    o_ref[0] = packed[:, :half]
    o_ref[1] = packed[:, half:]


def pack(window_rows, tiles, diag_inverse):
    _, cut, span = tiles.shape
    count = window_rows.shape[0] - 1
    panel = diag_inverse.shape[1]
    width = panel + span // count * (count * (count + 1) // 2)
    return pl.pallas_call(
        pack_kernel,
        out_shape=jax.ShapeDtypeStruct((2, cut, width // 2), tiles.dtype),
        in_specs=[
            pl.BlockSpec(memory_space=pltpu.SMEM),
            pl.BlockSpec(memory_space=pltpu.VMEM),
            pl.BlockSpec(memory_space=pl.ANY),
        ],
        out_specs=pl.BlockSpec(memory_space=pltpu.VMEM),
        scratch_shapes=[
            pltpu.VMEM((cut, panel), tiles.dtype),
            pltpu.SemaphoreType.DMA,
        ],
        name="pack_pieces",
    )(window_rows, tiles, diag_inverse)


def solve_kernel(rows_ref, pieces_ref, g_ref, o_ref, r_buf, d_buf, l_buf, r_sem, d_sem, l_sem):
    window, _, panel = r_buf.shape
    lanes = panel // SIDE
    right, inverse, lower = [], [], {}
    for k in range(window):
        copy = pltpu.make_async_copy(pieces_ref.at[rows_ref[k]], r_buf.at[k], r_sem.at[k])
        copy.start()
        right.append(copy)
        copy = pltpu.make_async_copy(
            g_ref.at[:, :, :, k, 0, :, pl.ds(0, panel)], d_buf.at[k], d_sem.at[k]
        )
        copy.start()
        inverse.append(copy)
        if k == 0:
            continue
        for j in range(k):
            half, lane = divmod(panel + (k * (k - 1) // 2 + j) * lanes, g_ref.shape[-1])
            for z in range(SIDE):
                copy = pltpu.make_async_copy(
                    g_ref.at[:, :, :, z, half, :, pl.ds(lane, lanes)],
                    l_buf.at[k - 1, :, :, :, :, pl.ds(j * panel + z * lanes, lanes)],
                    l_sem.at[k - 1, j, z],
                )
                copy.start()
                lower[k, j, z] = copy
    for k in range(window):
        right[k].wait()
        residual = r_buf[k].astype(jnp.float32)
        if k > 0:
            for j in range(k):
                for z in range(SIDE):
                    lower[k, j, z].wait()
            tiles = l_buf[k - 1, :, :, :, :, : k * panel].reshape(panel, k * panel)
            residual = residual - dot_nt(o_ref[:, : k * panel], tiles)
        inverse[k].wait()
        inv = d_buf[k].reshape(panel, panel)
        o_ref[:, k * panel : (k + 1) * panel] = dot_nt(residual.astype(jnp.bfloat16), inv).astype(
            jnp.bfloat16
        )


def solve(window_rows, pieces, spread):
    _, width, panel = pieces.shape
    window = window_rows.shape[0]
    cut = spread.shape[5]
    below = (window - 1) * panel
    return pl.pallas_call(
        solve_kernel,
        out_shape=jax.ShapeDtypeStruct((width, window * panel), pieces.dtype),
        in_specs=[
            pl.BlockSpec(memory_space=pltpu.SMEM),
            pl.BlockSpec(memory_space=pl.ANY),
            pl.BlockSpec(memory_space=pl.ANY),
        ],
        out_specs=pl.BlockSpec(memory_space=pltpu.VMEM),
        scratch_shapes=[
            pltpu.VMEM((window, width, panel), pieces.dtype),
            pltpu.VMEM((window, SIDE, SIDE, 2, cut, panel), pieces.dtype),
            pltpu.VMEM((window - 1, SIDE, SIDE, 2, cut, below), pieces.dtype),
            pltpu.SemaphoreType.DMA((window,)),
            pltpu.SemaphoreType.DMA((window,)),
            pltpu.SemaphoreType.DMA((window - 1, window - 1, SIDE)),
        ],
        name="solve_window",
    )(window_rows, pieces, spread)


def update_kernel(place_ref, mask_ref, r_ref, f_ref, w_ref, s_ref, o_ref, kept_ref):
    step = pl.program_id(0)

    @pl.when(step == 0)
    def _():
        kept_ref[...] = keep_present(mask_ref, f_ref, mask_ref.shape[1])

    removed = dot_nt(kept_ref[...], w_ref[...])
    o_ref[...] = (r_ref[...].astype(jnp.float32) - removed).astype(o_ref.dtype)

    @pl.when(step == place_ref[1])
    def _():
        rows = s_ref.shape[0]
        per = LANES // rows
        lane = pl.multiple_of(place_ref[0] // per * LANES, LANES)
        tile = w_ref[:, pl.ds(lane, LANES)].astype(jnp.float32).T
        mine = tile[:rows]
        for n in range(1, per):
            mine = jnp.where(place_ref[0] % per == n, tile[n * rows : (n + 1) * rows], mine)
        s_ref[...] = mine.astype(s_ref.dtype)


def update(place, tile_mask, right_side, factor, whole, nrow, ncol):
    panel, columns = right_side.shape
    step = columns // ncol
    rows = factor.shape[1] // nrow
    return pl.pallas_call(
        update_kernel,
        grid=(ncol,),
        out_shape=(
            jax.ShapeDtypeStruct((rows, step), whole.dtype),
            jax.ShapeDtypeStruct(right_side.shape, right_side.dtype),
        ),
        in_specs=[
            pl.BlockSpec(memory_space=pltpu.SMEM),
            pl.BlockSpec(memory_space=pltpu.SMEM),
            pl.BlockSpec((panel, step), lambda i: (0, i)),
            pl.BlockSpec(factor.shape, lambda i: (0, 0), pipeline_mode=pl.Buffered(1)),
            pl.BlockSpec((step, factor.shape[1]), lambda i: (i, 0)),
        ],
        out_specs=(
            pl.BlockSpec((rows, step), lambda i: (0, 0)),
            pl.BlockSpec((panel, step), lambda i: (0, i)),
        ),
        scratch_shapes=[pltpu.VMEM(factor.shape, factor.dtype)],
        name="update_panel",
    )(place, tile_mask, right_side, factor, whole)


def body(right_side, factor, diag_inverse, tile_mask, window_rows):
    panel = diag_inverse.shape[1]
    window = factor.shape[1] // panel
    columns = right_side.shape[1]
    ncol = lax.axis_size("col")
    nrow = lax.axis_size("row")
    ndev = nrow * ncol
    width = columns // ndev
    col_index = lax.axis_index("col")
    row_index = lax.axis_index("row")

    below = (window - 1) * panel
    cut = panel // nrow
    tiles = cut_tiles(factor, tile_mask, below, nrow, ncol)
    tiles = lax.all_to_all(
        tiles.reshape(ndev, cut, below // ncol), AXES, split_axis=0, concat_axis=0, tiled=True
    )
    pieces = lax.all_to_all(
        right_side.T.reshape(ndev, width, panel), AXES, split_axis=0, concat_axis=0, tiled=True
    )

    spread = gather_all(pack(window_rows, tiles, diag_inverse), 0)
    whole = solve(window_rows, pieces, spread)
    whole = gather_all(whole.reshape(2, width // 2, window * panel), 1).reshape(columns, window * panel)

    place = jnp.stack([row_index, col_index]).astype(jnp.int32)
    solution, updated = update(place, tile_mask, right_side, factor, whole, nrow, ncol)
    return (solution, updated)


def solution(mesh):
    in_specs = (
        P(AXES, None),
        P(AXES, None),
        P("col", None),
        P(AXES, None),
        P(),
    )
    out_specs = (P("row", "col"), P(AXES, None))
    return jax.shard_map(body, mesh=mesh, in_specs=in_specs, out_specs=out_specs, check_vma=False)
```

```python
import functools

import jax
import jax.numpy as jnp
from jax import lax
from jax.experimental import pallas as pl
from jax.experimental.pallas import tpu as pltpu
from jax.sharding import PartitionSpec as P

AXES = ("row", "col")
NT = (((1,), (1,)), ((), ()))
LANES = 128
SIDE = 4
SUBS = (0, -1, 1, 2)
ORDERS = ((2, 1, 0), (0, 2, 1), (1, 0, 2))


def dot_nt(a, b):
    return lax.dot_general(a, b, NT, preferred_element_type=jnp.float32)


def lane_parts(width):
    tiles = width // LANES
    sizes = [tiles // 3 + (1 if p < tiles % 3 else 0) for p in range(3)]
    starts = [sum(sizes[:p]) for p in range(3)]
    return [pl.ds(s * LANES, n * LANES) for s, n in zip(starts, sizes)]


def gather_kernel(x_ref, g_ref, local_sem, send_sem, recv_sem, side_send, side_recv):
    row, z = lax.axis_index("row"), lax.axis_index("col")
    x, y, core = row // 8, (row // 2) % 4, row % 2
    here = (x, y, z)
    parts = lane_parts(x_ref.shape[-1])

    def device(coords, c):
        return ((coords[0] * 4 + coords[1]) * 2 + c, coords[2])

    def shifted(axis, step):
        coords = list(here)
        coords[axis] = (coords[axis] + step + SIDE) % SIDE
        return coords

    partner = device(here, 1 - core)
    barrier = pltpu.get_barrier_semaphore()
    for axis in range(3):
        for step in (1, -1):
            pl.semaphore_signal(
                barrier, inc=1, device_id=device(shifted(axis, step), core),
                device_id_type=pl.DeviceIdType.MESH,
            )
    pl.semaphore_signal(barrier, inc=1, device_id=partner, device_id_type=pl.DeviceIdType.MESH)
    pl.semaphore_wait(barrier, 7)

    def block(p, f, offset, half=None, sub=None):
        order = ORDERS[p]
        idx = []
        for axis in range(3):
            if axis == order[f]:
                idx.append(pl.ds((here[axis] + offset + SIDE) % SIDE, 1))
            elif axis in order[:f] and (sub is None or axis != order[f - 1]):
                idx.append(pl.ds(0, SIDE))
            else:
                idx.append(pl.ds((here[axis] + (sub or 0) + SIDE) % SIDE if axis in order[:f] else here[axis], 1))
        halves = pl.ds(0, 2) if half is None else pl.ds(half, 1)
        return g_ref.at[idx[0], idx[1], pl.ds(core, 1), idx[2], halves, :, parts[p]]

    started = []

    def send(p, f, n, stage, way, src, dst):
        to = device(shifted(ORDERS[p][f], 1 if way == 0 else -1), core)
        copy = pltpu.make_async_remote_copy(
            src_ref=src, dst_ref=dst, send_sem=send_sem.at[p, f, n, stage, way],
            recv_sem=recv_sem.at[p, f, n, stage, way], device_id=to,
            device_id_type=pl.DeviceIdType.MESH,
        )
        copy.start()
        started.append(copy)
        return copy

    sides = []

    def hand_over(p, n, src, dst):
        copy = pltpu.make_async_remote_copy(
            src_ref=src, dst_ref=dst, send_sem=side_send.at[p, n], recv_sem=side_recv.at[p, n],
            device_id=partner, device_id_type=pl.DeviceIdType.MESH,
        )
        copy.start()
        sides.append(copy)

    first = {}

    def send_halves(p, f, n):
        sub = SUBS[n] if f > 0 else None
        for stage in range(2):
            for way in (0, 1):
                half = way if stage == 0 else 1 - way
                dst = block(p, f, 0, half, sub)
                if f == 0 or (f == 1 and n == 0):
                    src = x_ref.at[:, :, :, :, pl.ds(half, 1), :, parts[p]]
                else:
                    src = dst
                first[p, f, n, stage, way] = send(p, f, n, stage, way, src, dst)

    for p in range(3):
        send_halves(p, 0, 0)
    keep = pltpu.make_async_copy(
        x_ref, g_ref.at[pl.ds(x, 1), pl.ds(y, 1), pl.ds(core, 1), pl.ds(z, 1)], local_sem
    )
    keep.start()
    for p in range(3):
        hand_over(p, 0, x_ref.at[:, :, :, :, :, :, parts[p]], block(p, 0, 0))
    sides_of = ((0, -1), (1, 1))
    for f in range(3):
        if f == 1:
            keep.wait()
        if f < 2:
            for p in range(3):
                send_halves(p, f + 1, 0)
        second = {}
        for n in range(len(SUBS) if f > 0 else 1):
            sub = SUBS[n] if f > 0 else None
            for p in range(3):
                for way, offset in sides_of:
                    first[p, f, n, 0, way].wait_recv()
                    piece = block(p, f, offset, way, sub)
                    second[p, n, way] = send(p, f, n, 2, way, piece, piece)
            for p in range(3):
                for way, offset in sides_of:
                    first[p, f, n, 1, way].wait_recv()
                    if f == 2:
                        piece = block(p, f, offset, None, sub)
                        hand_over(p, 7 + 4 * way + n, piece, piece)
        if f == 2:
            for n in range(len(SUBS)):
                for p in range(3):
                    for way in (0, 1):
                        second[p, n, way].wait_recv()
                    piece = block(p, f, 2, None, SUBS[n])
                    hand_over(p, 15 + n, piece, piece)
            break
        for p in range(3):
            if f < 2:
                send_halves(p, f + 1, 1)
                send_halves(p, f + 1, 2)
            for way, offset in sides_of:
                whole = block(p, f, offset)
                hand_over(p, 3 * f + 1 + way, whole, whole)
        for p in range(3):
            for key, copy in second.items():
                if key[0] == p:
                    copy.wait_recv()
            if f < 2:
                send_halves(p, f + 1, 3)
            far = block(p, f, 2)
            hand_over(p, 3 * f + 3, far, far)
    for copy in started:
        copy.wait_send()
    for copy in sides:
        copy.wait()


def gather_all(shard, collective_id):
    halves, rows, width = shard.shape
    return pl.pallas_call(
        gather_kernel,
        out_shape=jax.ShapeDtypeStruct((SIDE, SIDE, 2, SIDE, halves, rows, width), shard.dtype),
        in_specs=[pl.BlockSpec(memory_space=pltpu.VMEM)],
        out_specs=pl.BlockSpec(memory_space=pltpu.HBM),
        scratch_shapes=[
            pltpu.SemaphoreType.DMA,
            pltpu.SemaphoreType.DMA((3, 3, 4, 3, 2)),
            pltpu.SemaphoreType.DMA((3, 3, 4, 3, 2)),
            pltpu.SemaphoreType.DMA((3, 19)),
            pltpu.SemaphoreType.DMA((3, 19)),
        ],
        compiler_params=pltpu.CompilerParams(collective_id=collective_id, has_side_effects=True),
        name="gather_all_%d" % width,
    )(shard.reshape(1, 1, 1, 1, halves, rows, width))


def keep_present(mask_ref, f_ref, count):
    panel = f_ref.shape[1] // count
    tiles = []
    for j in range(count):
        tile = f_ref[:, j * panel : (j + 1) * panel]
        tiles.append(jnp.where(mask_ref[0, j] > 0, tile, jnp.zeros_like(tile)))
    return jnp.concatenate(tiles, axis=1)


def cut_kernel(mask_ref, f_ref, o_ref):
    groups, ncol, cut, span = o_ref.shape
    count = mask_ref.shape[1] - 1
    panel, lanes = f_ref.shape[1] // count, span // count
    kept = keep_present(mask_ref, f_ref, count)
    for g in range(groups):
        for c in range(ncol):
            rows = kept[g * cut : (g + 1) * cut]
            o_ref[g, c] = jnp.concatenate(
                [rows[:, j * panel + c * lanes : j * panel + (c + 1) * lanes] for j in range(count)],
                axis=1,
            )


def cut_tiles(factor, tile_mask, below, nrow, ncol):
    panel = factor.shape[0]
    cut, span, steps = panel // nrow, below // ncol, 4
    return pl.pallas_call(
        cut_kernel,
        grid=(steps,),
        out_shape=jax.ShapeDtypeStruct((nrow, ncol, cut, span), factor.dtype),
        in_specs=[
            pl.BlockSpec(memory_space=pltpu.SMEM),
            pl.BlockSpec((panel // steps, below), lambda i: (i, 0)),
        ],
        out_specs=pl.BlockSpec((nrow // steps, ncol, cut, span), lambda i: (i, 0, 0, 0)),
        name="cut_tiles",
    )(tile_mask, factor)


def pack_kernel(rows_ref, tiles_ref, inverse_ref, o_ref, d_buf, sem):
    count = rows_ref.shape[0] - 1
    _, cut, span = tiles_ref.shape
    lanes = span // count
    start = pl.multiple_of(lax.axis_index("row") * cut, cut)
    copy = pltpu.make_async_copy(inverse_ref.at[pl.ds(start, cut)], d_buf, sem)
    copy.start()
    pieces = [tiles_ref[rows_ref[k]][:, : k * lanes] for k in range(1, count + 1)]
    copy.wait()
    packed = [d_buf[...]] + pieces
    packed = jnp.concatenate(packed, axis=1)
    half = o_ref.shape[-1]
    o_ref[0] = packed[:, :half]
    o_ref[1] = packed[:, half:]


def pack(window_rows, tiles, diag_inverse):
    _, cut, span = tiles.shape
    count = window_rows.shape[0] - 1
    panel = diag_inverse.shape[1]
    width = panel + span // count * (count * (count + 1) // 2)
    return pl.pallas_call(
        pack_kernel,
        out_shape=jax.ShapeDtypeStruct((2, cut, width // 2), tiles.dtype),
        in_specs=[
            pl.BlockSpec(memory_space=pltpu.SMEM),
            pl.BlockSpec(memory_space=pltpu.VMEM),
            pl.BlockSpec(memory_space=pl.ANY),
        ],
        out_specs=pl.BlockSpec(memory_space=pltpu.VMEM),
        scratch_shapes=[
            pltpu.VMEM((cut, panel), tiles.dtype),
            pltpu.SemaphoreType.DMA,
        ],
        name="pack_pieces",
    )(window_rows, tiles, diag_inverse)


def solve_kernel(rows_ref, pieces_ref, g_ref, o_ref, r_buf, d_buf, l_buf, r_sem, d_sem, l_sem):
    window, _, panel = r_buf.shape
    lanes = panel // SIDE
    right, inverse, lower = [], [], {}
    for k in range(window):
        copy = pltpu.make_async_copy(pieces_ref.at[rows_ref[k]], r_buf.at[k], r_sem.at[k])
        copy.start()
        right.append(copy)
        copy = pltpu.make_async_copy(
            g_ref.at[:, :, :, k, 0, :, pl.ds(0, panel)], d_buf.at[k], d_sem.at[k]
        )
        copy.start()
        inverse.append(copy)
        if k == 0:
            continue
        for j in range(k):
            half, lane = divmod(panel + (k * (k - 1) // 2 + j) * lanes, g_ref.shape[-1])
            for z in range(SIDE):
                copy = pltpu.make_async_copy(
                    g_ref.at[:, :, :, z, half, :, pl.ds(lane, lanes)],
                    l_buf.at[k - 1, :, :, :, :, pl.ds(j * panel + z * lanes, lanes)],
                    l_sem.at[k - 1, j, z],
                )
                copy.start()
                lower[k, j, z] = copy
    for k in range(window):
        right[k].wait()
        residual = r_buf[k].astype(jnp.float32)
        if k > 0:
            for j in range(k):
                for z in range(SIDE):
                    lower[k, j, z].wait()
            tiles = l_buf[k - 1, :, :, :, :, : k * panel].reshape(panel, k * panel)
            residual = residual - dot_nt(o_ref[:, : k * panel], tiles)
        inverse[k].wait()
        inv = d_buf[k].reshape(panel, panel)
        o_ref[:, k * panel : (k + 1) * panel] = dot_nt(residual.astype(jnp.bfloat16), inv).astype(
            jnp.bfloat16
        )


def solve(window_rows, pieces, spread):
    _, width, panel = pieces.shape
    window = window_rows.shape[0]
    cut = spread.shape[5]
    below = (window - 1) * panel
    return pl.pallas_call(
        solve_kernel,
        out_shape=jax.ShapeDtypeStruct((width, window * panel), pieces.dtype),
        in_specs=[
            pl.BlockSpec(memory_space=pltpu.SMEM),
            pl.BlockSpec(memory_space=pl.ANY),
            pl.BlockSpec(memory_space=pl.ANY),
        ],
        out_specs=pl.BlockSpec(memory_space=pltpu.VMEM),
        scratch_shapes=[
            pltpu.VMEM((window, width, panel), pieces.dtype),
            pltpu.VMEM((window, SIDE, SIDE, 2, cut, panel), pieces.dtype),
            pltpu.VMEM((window - 1, SIDE, SIDE, 2, cut, below), pieces.dtype),
            pltpu.SemaphoreType.DMA((window,)),
            pltpu.SemaphoreType.DMA((window,)),
            pltpu.SemaphoreType.DMA((window - 1, window - 1, SIDE)),
        ],
        name="solve_window",
    )(window_rows, pieces, spread)


def update_kernel(place_ref, mask_ref, r_ref, f_ref, w_ref, s_ref, o_ref, kept_ref):
    step = pl.program_id(0)

    @pl.when(step == 0)
    def _():
        kept_ref[...] = keep_present(mask_ref, f_ref, mask_ref.shape[1])

    removed = dot_nt(kept_ref[...], w_ref[...])
    o_ref[...] = (r_ref[...].astype(jnp.float32) - removed).astype(o_ref.dtype)

    @pl.when(step == place_ref[1])
    def _():
        rows = s_ref.shape[0]
        per = LANES // rows
        lane = pl.multiple_of(place_ref[0] // per * LANES, LANES)
        tile = w_ref[:, pl.ds(lane, LANES)].astype(jnp.float32).T
        mine = tile[:rows]
        for n in range(1, per):
            mine = jnp.where(place_ref[0] % per == n, tile[n * rows : (n + 1) * rows], mine)
        s_ref[...] = mine.astype(s_ref.dtype)


def update(place, tile_mask, right_side, factor, whole, nrow, ncol):
    panel, columns = right_side.shape
    step = columns // ncol
    rows = factor.shape[1] // nrow
    return pl.pallas_call(
        update_kernel,
        grid=(ncol,),
        out_shape=(
            jax.ShapeDtypeStruct((rows, step), whole.dtype),
            jax.ShapeDtypeStruct(right_side.shape, right_side.dtype),
        ),
        in_specs=[
            pl.BlockSpec(memory_space=pltpu.SMEM),
            pl.BlockSpec(memory_space=pltpu.SMEM),
            pl.BlockSpec((panel, step), lambda i: (0, i)),
            pl.BlockSpec(factor.shape, lambda i: (0, 0), pipeline_mode=pl.Buffered(1)),
            pl.BlockSpec((step, factor.shape[1]), lambda i: (i, 0)),
        ],
        out_specs=(
            pl.BlockSpec((rows, step), lambda i: (0, 0)),
            pl.BlockSpec((panel, step), lambda i: (0, i)),
        ),
        scratch_shapes=[pltpu.VMEM(factor.shape, factor.dtype)],
        name="update_panel",
    )(place, tile_mask, right_side, factor, whole)


def body(right_side, factor, diag_inverse, tile_mask, window_rows):
    panel = diag_inverse.shape[1]
    window = factor.shape[1] // panel
    columns = right_side.shape[1]
    ncol = lax.axis_size("col")
    nrow = lax.axis_size("row")
    ndev = nrow * ncol
    width = columns // ndev
    col_index = lax.axis_index("col")
    row_index = lax.axis_index("row")

    below = (window - 1) * panel
    cut = panel // nrow
    tiles = cut_tiles(factor, tile_mask, below, nrow, ncol)
    tiles = lax.all_to_all(
        tiles.reshape(ndev, cut, below // ncol), AXES, split_axis=0, concat_axis=0, tiled=True
    )
    pieces = lax.all_to_all(
        right_side.T.reshape(ndev, width, panel), AXES, split_axis=0, concat_axis=0, tiled=True
    )

    spread = gather_all(pack(window_rows, tiles, diag_inverse), 0)
    whole = solve(window_rows, pieces, spread)
    whole = gather_all(whole.reshape(2, width // 2, window * panel), 1).reshape(columns, window * panel)

    place = jnp.stack([row_index, col_index]).astype(jnp.int32)
    solution, updated = update(place, tile_mask, right_side, factor, whole, nrow, ncol)
    return (solution, updated)


def solution(mesh):
    in_specs = (
        P(AXES, None),
        P(AXES, None),
        P("col", None),
        P(AXES, None),
        P(),
    )
    out_specs = (P("row", "col"), P(AXES, None))
    return jax.shard_map(body, mesh=mesh, in_specs=in_specs, out_specs=out_specs, check_vma=False)
```
